512 devices in a mesh: vox: 8 (over x, z_hi), row: 16 (over z_lo, core), wl: 4 (over y).
Axes of the slice: x: 4, y: 4, z: 16 (z_hi: 2, z_lo: 8; z = z_hi * 8 + z_lo), core: 2. Of those that a mesh axis runs over, the one named last changes fastest.
Arguments:
- jacobian: bfloat16 [8192, 5120], P(('row', 'wl'), 'vox'), may hold values from -0.078125 to 0.078125
- extinction: float32 [4, 2], replicated, may hold values from 0.3 to 3
- prior_var: float32 [2, 5120], P(None, 'vox'), may hold values from 0.1 to 10
Outputs:
- gram: float32 [8192, 8192], P(('row', 'wl'), 'vox')
The draws below stay inside these ranges and needn't reach their ends.
All inputs are finite; a program needn't handle non-finite values.
Results may differ from the reference program's by a relative error of at most 0.005.
Values may be sent and summed in bfloat16 or wider, within the bound.
A program may use at most 128 MiB of HBM per device.

```python
import math
import jax
import jax.numpy as jnp
from jax import lax

WL = 4
CHROM = 2
ROW_DEV = 128
GRAM = 8192
VOX = 5120


def levels(rng, shape, cuts, smallest, high):
    def one(axis_at, parts):
        draws = jax.random.uniform(jax.random.fold_in(jax.random.fold_in(rng, 6), axis_at), (parts,), jnp.float32, smallest / len(cuts), high / len(cuts))
        return jnp.repeat(jnp.exp(draws), shape[axis_at] // parts).reshape((-1,) + (1,) * (len(shape) - axis_at - 1))

    level = one(*cuts[0])
    for cut in cuts[1:]:
        level = level * one(*cut)
    return level


def gaussian(stream_key, shape, scale, limit, split=(), held_as=jnp.bfloat16):
    entries = jax.random.normal(stream_key, shape, jnp.float32) * scale
    if len(split) > 0:
        entries = levels(stream_key, shape, split, -0.22, 0.18) * entries
    return jnp.clip(entries, min=-limit, max=limit).astype(held_as)


def setup_inputs(seed: int = 0) -> dict:
    keys = jax.random.split(jax.random.key(seed), 4)
    jacobian = gaussian(keys[0], (GRAM, VOX), VOX ** -0.5, 0.078125, ((0, 64), (1, 8)))
    extinction = jnp.clip(jnp.exp(jax.random.uniform(keys[1], (WL, CHROM), jnp.float32, math.log(0.3), math.log(3.0))), 0.3, 3.0)
    prior_var = jnp.clip(jnp.exp(math.log(10.0) - 4.6051702 * jax.random.uniform(keys[2], (CHROM, VOX), jnp.float32) ** levels(keys[2], (CHROM, VOX), ((1, 8),), -0.2, 0.2)), 0.1, 10.0)
    return dict(jacobian=jacobian, extinction=extinction, prior_var=prior_var)


def reference(jacobian, extinction, prior_var):
    order = jacobian.shape[0]
    voxels = jacobian.shape[1]
    tiles = order // (ROW_DEV * WL)
    waves = (jnp.arange(order, dtype=jnp.int32) // ROW_DEV) % WL
    jac_wide = jacobian.astype(jnp.float32)
    result = jnp.zeros((tiles, WL, ROW_DEV, order), jnp.float32)
    for wave_index in range(WL):
        table = jnp.dot(extinction * extinction[wave_index][None, :], prior_var, precision=lax.Precision.HIGHEST)
        weights = table[waves]
        scaled = jac_wide * weights
        picked = jac_wide.reshape(tiles, WL, ROW_DEV, voxels)[:, wave_index].reshape(tiles * ROW_DEV, voxels)
        block_rows = jnp.dot(picked, scaled.T, precision=lax.Precision.HIGHEST, preferred_element_type=jnp.float32)
        result = result.at[:, wave_index].set(block_rows.reshape(tiles, ROW_DEV, order))
    return jnp.tril(result.reshape(order, order))
```

```python
import functools
import jax
import jax.numpy as jnp
from jax import lax
from jax.experimental import pallas as pl
from jax.experimental.pallas import tpu as pltpu
from jax.sharding import PartitionSpec as P

MESH = pl.DeviceIdType.MESH
NT = (((1,), (1,)), ((), ()))


def rem(a, n):
    return lax.rem(a, jnp.int32(n))


def div(a, n):
    return lax.div(a, jnp.int32(n))


def kernel(
    pieces,
    j_ref, ext_ref, pri_ref, out_ref,
    zb, cb, rb, prx, sh, sl, part, ra, rx, fin, yb,
    zs, zr, cs, cr, ys, yr, as_, ar, xs, xr, fs, fr, ps, pr,
):
    rows, vox = j_ref.shape
    step = rows // pieces
    half_rows = rows // 2
    v = lax.axis_index("vox")
    r = lax.axis_index("row")
    y = lax.axis_index("wl")
    x, h = div(v, 2), rem(v, 2)
    i, c = div(r, 2), rem(r, 2)
    z = h * 8 + i
    kind = rem(i + h, 2)

    def at(x_=None, z_=None, y_=None, c_=None):
        x_ = x if x_ is None else x_
        z_ = z if z_ is None else z_
        y_ = y if y_ is None else y_
        c_ = c if c_ is None else c_
        return {"vox": x_ * 2 + div(z_, 8), "row": rem(z_, 8) * 2 + c_, "wl": y_}

    x_next, x_prev = at(x_=rem(x + 1, 4)), at(x_=rem(x + 3, 4))
    y_next, y_prev, y_far = at(y_=rem(y + 1, 4)), at(y_=rem(y + 3, 4)), at(y_=rem(y + 2, 4))
    z_next, z_prev, z_far = at(z_=rem(z + 1, 16)), at(z_=rem(z + 15, 16)), at(z_=rem(z + 8, 16))
    other = at(c_=1 - c)
    z_to = (z_next, z_prev)

    barrier = pltpu.get_barrier_semaphore()
    partners = (x_next, x_prev, y_next, y_prev, y_far, z_next, z_prev, z_far, other)
    for device in partners:
        pl.semaphore_signal(barrier, inc=1, device_id=device, device_id_type=MESH)
    pl.semaphore_wait(barrier, len(partners))

    def send(src, dst, ssem, rsem, device):
        return pltpu.make_async_remote_copy(
            src_ref=src, dst_ref=dst, send_sem=ssem, recv_sem=rsem,
            device_id=device, device_id_type=MESH,
        )

    def kind_at(way, d):
        s = rem(z + 16 - d, 16) if way == 0 else rem(z + d, 16)
        return rem(div(s, 8) + s, 2)

    def z_copy(way, d, p, src):
        cut = pl.ds(p * step, step)
        return send(
            src.at[cut, :], zb.at[way, d, cut, :], zs.at[way, d, p], zr.at[way, d, p], z_to[way]
        )

    def target(delta):
        return rem(div(i - delta - h, 2) + 4 - x, 4)

    def c_copy(where, src, dx):
        return send(src, cb.at[dx, where], cs.at[where, dx], cr.at[where, dx], other)

    def y_copy(where, q, s, src):
        cut = pl.ds(q * half_rows, half_rows)
        return send(
            src.at[cut, :], rb.at[s - 1, where, cut, :],
            ys.at[where, q, s - 1], yr.at[where, q, s - 1],
            y_prev if s == 3 or (s == 2 and q == 1) else y_next,
        )

    def y_relay(where, q):
        s = 1 if q == 0 else 3
        y_copy(where, q, s, rb.at[s - 1, where]).wait_recv()
        y_copy(where, q, 2, rb.at[s - 1, where]).start()

    p_copy = send(pri_ref, prx, ps, pr, z_far)
    for way in (0, 1):
        @pl.when(kind == way)
        def _():
            for p in range(pieces):
                z_copy(way, 1, p, j_ref).start()
    for q in (0, 1):
        for s in (1, 3):
            y_copy(0, q, s, j_ref).start()
    p_copy.start()

    @pl.when(kind == 0)
    def _():
        c_copy(0, j_ref, target(0)).start()
        zb[0, 0] = j_ref[...]

    def hop(d, carry):
        for way in (0, 1):
            @pl.when(kind_at(way, d) == way)
            def _():
                for p in range(pieces):
                    z_copy(way, d, p, zb.at[way, d]).wait_recv()
                    @pl.when(d < 8)
                    def _():
                        z_copy(way, d + 1, p, zb.at[way, d]).start()
                    if (p + 1) % (pieces // 2) == 0:
                        q = (p + 1) // (pieces // 2) - 1
                        @pl.when(d == 8)
                        def _():
                            y_copy(1, q, 1, zb.at[way, d]).start()
                            y_copy(1, q, 3, zb.at[way, d]).start()
                delta = d if way == 0 else 8 - d
                @pl.when(delta <= i)
                def _():
                    c_copy(way, zb.at[way, d], target(delta)).start()

        @pl.when(d == 3)
        def _():
            y_relay(0, 0)
            y_relay(0, 1)
        return carry

    lax.fori_loop(1, 9, hop, 0)

    def weight(pri, a):
        w0 = ext_ref[a, 0] * ext_ref[y, 0]
        w1 = ext_ref[a, 1] * ext_ref[y, 1]
        return pri[0:1, :] * w0 + pri[1:2, :] * w1

    def scale(where, s, src, pri):
        value = src.astype(jnp.float32) * weight(pri, rem(y + 4 - s, 4))
        high = value.astype(jnp.bfloat16)
        cut = pl.ds(s * rows, rows)
        sh[where, cut, :] = high
        sl[where, cut, :] = (value - high.astype(jnp.float32)).astype(jnp.bfloat16)

    def active(dx):
        return rem(x + dx, 4) * 2 + h <= i

    def columns(where, dx):
        j = rem(x + dx, 4) * 2 + h
        delta = i - j
        own = zb[0, delta] if where == 0 else zb[1, 8 - delta]
        return jnp.concatenate([own, cb[dx, where]], axis=0)

    def product(where, dx):
        cols = columns(where, dx)
        return lax.dot_general(
            sh[where], cols, NT, preferred_element_type=jnp.float32
        ) + lax.dot_general(sl[where], cols, NT, preferred_element_type=jnp.float32)

    for q in (0, 1):
        y_copy(0, q, 1 if q == 1 else 3, j_ref).wait_recv()
        y_copy(0, q, 2, j_ref).wait_recv()
    scale(0, 0, j_ref[...], pri_ref[...])
    for s in (1, 2, 3):
        scale(0, s, rb[s - 1, 0], pri_ref[...])
    for dx in (2, 1, 3, 0):
        @pl.when(active(dx))
        def _():
            c_copy(0, j_ref, dx).wait_recv()
            part[dx] = product(0, dx)

    y_relay(1, 0)
    y_relay(1, 1)
    p_copy.wait_recv()
    scale(1, 0, zb[1 - kind, 8], prx[...])
    y_copy(1, 1, 1, j_ref).wait_recv()
    scale(1, 1, rb[0, 1], prx[...])
    y_copy(1, 0, 3, j_ref).wait_recv()
    scale(1, 3, rb[2, 1], prx[...])
    for q in (0, 1):
        y_copy(1, q, 2, j_ref).wait_recv()
    scale(1, 2, rb[1, 1], prx[...])

    wide = rows * 2

    def a_copy(k):
        return send(
            part.at[2, pl.ds(k * wide, wide), :], ra.at[k], as_.at[k], ar.at[k],
            x_next if k == 0 else x_prev,
        )

    def x_copy(k, q):
        cut = pl.ds(q * wide, wide)
        return send(
            part.at[1 if k == 0 else 3, cut, :], rx.at[k, cut, :], xs.at[k, q], xr.at[k, q],
            x_next if k == 0 else x_prev,
        )

    for dx in (2, 1, 3, 0):
        @pl.when(active(dx))
        def _():
            c_copy(1, j_ref, dx).wait_recv()
            part[dx] = part[dx] + product(1, dx)
            if dx == 2:
                a_copy(0).start()
                a_copy(1).start()
            if dx == 1:
                x_copy(0, 1).start()
            if dx == 3:
                x_copy(1, 0).start()
    for k, dx in ((0, 1), (1, 3)):
        @pl.when(active(dx))
        def _():
            a_copy(k).wait_recv()
            cut = pl.ds(k * wide, wide)
            part[dx, cut, :] = part[dx, cut, :] + ra[k]
            x_copy(k, k).start()

    def f_copy(s):
        cut = pl.ds(s * rows, rows)
        device = {1: y_prev, 2: y_far, 3: y_next}[s]
        return send(fin.at[cut, :], yb.at[s - 1], fs.at[s - 1], fr.at[s - 1], device)

    j_own = x * 2 + h
    mine = j_own <= i

    @pl.when(mine)
    def _():
        for q in (0, 1):
            x_copy(0, q).wait_recv()
            x_copy(1, q).wait_recv()
            cut = pl.ds(q * wide, wide)
            fin[cut, :] = part[0, cut, :] + rx[0, cut, :] + rx[1, cut, :]
            for s in ((1,) if q == 0 else (2, 3)):
                f_copy(s).start()

        def place(s, value):
            source = rem(y + s, 4)
            row = ((i * 2 + c) * 4 + y) * rows + lax.broadcasted_iota(jnp.int32, (rows, rows), 0)
            lane = lax.broadcasted_iota(jnp.int32, (rows, rows), 1)
            for k in (0, 1):
                block = (c if k == 0 else 1 - c) * 4 + source
                col = j_own * (rows * 8) + block * rows + lane
                piece = value[:, k * rows:(k + 1) * rows]
                out_ref[:, pl.ds(pl.multiple_of(block * rows, rows), rows)] = jnp.where(
                    col <= row, piece, 0.0
                )

        place(0, fin[0:rows, :])
        for s in (1, 3, 2):
            f_copy(s).wait_recv()
            place(s, yb[s - 1])

    @pl.when(j_own > i)
    def _():
        out_ref[...] = jnp.zeros_like(out_ref)

    p_copy.wait_send()

    def drain(d, carry):
        for way in (0, 1):
            @pl.when(kind_at(way, d - 1) == way)
            def _():
                for p in range(pieces):
                    z_copy(way, d, p, zb.at[way, d]).wait_send()
        return carry

    lax.fori_loop(1, 9, drain, 0)
    for where in (0, 1):
        for q in (0, 1):
            for s in (1, 2, 3):
                y_copy(where, q, s, j_ref).wait_send()
    for dx in range(4):
        @pl.when(active(dx))
        def _():
            for where in (0, 1):
                c_copy(where, j_ref, dx).wait_send()
            if dx == 2:
                a_copy(0).wait_send()
                a_copy(1).wait_send()
            if dx == 1 or dx == 3:
                for q in (0, 1):
                    x_copy(0 if dx == 1 else 1, q).wait_send()

    @pl.when(mine)
    def _():
        for s in (1, 2, 3):
            f_copy(s).wait_send()


def on_device(pieces, jacobian, extinction, prior_var):
    rows, vox = jacobian.shape
    width = rows * 8
    dma = pltpu.SemaphoreType.DMA
    vmem = pltpu.VMEM
    f32, bf16 = jnp.float32, jnp.bfloat16
    return pl.pallas_call(
        functools.partial(kernel, pieces),
        out_shape=jax.ShapeDtypeStruct((rows, width), f32),
        in_specs=[
            pl.BlockSpec(memory_space=pltpu.VMEM),
            pl.BlockSpec(memory_space=pltpu.SMEM),
            pl.BlockSpec(memory_space=pltpu.VMEM),
        ],
        out_specs=pl.BlockSpec(memory_space=pltpu.VMEM),
        scratch_shapes=[
            vmem((2, 9, rows, vox), bf16),
            vmem((4, 2, rows, vox), bf16),
            vmem((3, 2, rows, vox), bf16),
            vmem((2, vox), f32),
            vmem((2, rows * 4, vox), bf16),
            vmem((2, rows * 4, vox), bf16),
            vmem((4, rows * 4, rows * 2), f32),
            vmem((2, rows * 2, rows * 2), f32),
            vmem((2, rows * 4, rows * 2), f32),
            vmem((rows * 4, rows * 2), f32),
            vmem((3, rows, rows * 2), f32),
            dma((2, 9, pieces)), dma((2, 9, pieces)),
            dma((2, 4)), dma((2, 4)),
            dma((2, 2, 3)), dma((2, 2, 3)),
            dma((2,)), dma((2,)),
            dma((2, 2)), dma((2, 2)),
            dma((3,)), dma((3,)),
            dma, dma,
        ],
        compiler_params=pltpu.CompilerParams(
            collective_id=0, has_side_effects=True, vmem_limit_bytes=48 * 2**20
        ),
    )(jacobian, extinction, prior_var)


def solution(mesh):
    return jax.shard_map(
        functools.partial(on_device, 4),
        mesh=mesh,
        in_specs=(P(("row", "wl"), "vox"), P(), P(None, "vox")),
        out_specs=P(("row", "wl"), "vox"),
        check_vma=False,
    )
```

```python
import functools
import jax
import jax.numpy as jnp
from jax import lax
from jax.experimental import pallas as pl
from jax.experimental.pallas import tpu as pltpu
from jax.sharding import PartitionSpec as P

MESH = pl.DeviceIdType.MESH
NT = (((1,), (1,)), ((), ()))


def rem(a, n):
    return lax.rem(a, jnp.int32(n))


def div(a, n):
    return lax.div(a, jnp.int32(n))


def kernel(
    pieces,
    j_ref, ext_ref, pri_ref, out_ref,
    zb, cb, rb, ext, pri, tab, sh, sl, part, ra, rx, fin, yb, fb,
    zs, zr, cs, cr, ys, yr, as_, ar, xs, xr, fs, fr, gs, gr, ps, pr, ls,
):
    rows, vox = j_ref.shape
    step = rows // pieces
    half_rows = rows // 2
    v = lax.axis_index("vox")
    r = lax.axis_index("row")
    y = lax.axis_index("wl")
    x, h = div(v, 2), rem(v, 2)
    i, c = div(r, 2), rem(r, 2)
    z = h * 8 + i
    role = rem(i + h, 2)
    kind = rem(i + h + div(i, 7) * c, 2)

    def at(x_=None, z_=None, y_=None, c_=None):
        x_ = x if x_ is None else x_
        z_ = z if z_ is None else z_
        y_ = y if y_ is None else y_
        c_ = c if c_ is None else c_
        return {"vox": x_ * 2 + div(z_, 8), "row": rem(z_, 8) * 2 + c_, "wl": y_}

    x_next, x_prev = at(x_=rem(x + 1, 4)), at(x_=rem(x + 3, 4))
    y_next, y_prev = at(y_=rem(y + 1, 4)), at(y_=rem(y + 3, 4))
    z_next, z_prev = at(z_=rem(z + 1, 16)), at(z_=rem(z + 15, 16))
    z_up, z_down = at(z_=rem(z + 4, 16)), at(z_=rem(z + 12, 16))
    other = at(c_=1 - c)

    barrier = pltpu.get_barrier_semaphore()
    partners = (z_up, z_down, z_next, z_prev, y_next, y_prev, x_next, x_prev, other)
    for device in partners:
        pl.semaphore_signal(barrier, inc=1, device_id=device, device_id_type=MESH)
    loads = [
        pltpu.make_async_copy(src, dst, ls.at[k])
        for k, (src, dst) in enumerate(((j_ref, zb.at[0, 0]), (ext_ref, ext), (pri_ref, pri.at[0])))
    ]
    for load in loads:
        load.start()
    loads[0].wait()
    pl.semaphore_wait(barrier, len(partners))

    def send(src, dst, ssem, rsem, device):
        return pltpu.make_async_remote_copy(
            src_ref=src, dst_ref=dst, send_sem=ssem, recv_sem=rsem,
            device_id=device, device_id_type=MESH,
        )

    def source(way, d):
        s = rem(z + 16 - d, 16) if way == 0 else rem(z + d, 16)
        place = rem(s, 8)
        return rem(div(s, 8) + place + div(place, 7) * c, 2)

    def has(way, d):
        return source(way, d) == way

    def sends(way, d):
        return source(way, d - 1) == way

    def z_copy(way, d, p):
        cut = pl.ds(p * step, step)
        src = zb.at[0, 0] if d == 1 else zb.at[way, d - 1]
        device = z_next if way == 0 else z_prev
        return send(
            src.at[cut, :], zb.at[way, d, cut, :], zs.at[way, d, p], zr.at[way, d, p], device
        )

    def target(delta):
        return rem(div(i - delta - h, 2) + 4 - x, 4)

    def c_copy(where, src, dx):
        return send(src, cb.at[dx, where], cs.at[where, dx], cr.at[where, dx], other)

    def y_copy(where, q, s, src):
        cut = pl.ds(q * half_rows, half_rows)
        return send(
            src.at[cut, :], rb.at[s - 1, where, cut, :],
            ys.at[where, q, s - 1], yr.at[where, q, s - 1],
            y_prev if s == 3 or (s == 2 and q == 1) else y_next,
        )

    def y_relay(where, q):
        s = 1 if q == 0 else 3
        y_copy(where, q, s, rb.at[s - 1, where]).wait_recv()
        y_copy(where, q, 2, rb.at[s - 1, where]).start()

    def p_copy(k):
        return send(pri_ref if k == 0 else pri.at[1], pri.at[k + 1], ps.at[k], pr.at[k], z_up)

    def start_z(way, d, p):
        @pl.when(sends(way, d))
        def _():
            z_copy(way, d, p).start()

    for p in range(pieces):
        start_z(0, 1, p)
        start_z(1, 1, p)
    p_copy(0).start()
    for q in (0, 1):
        for s in (1, 3):
            y_copy(0, q, s, zb.at[0, 0]).start()

    @pl.when(role == 0)
    def _():
        c_copy(0, zb.at[0, 0], target(0)).start()

    def take(way, d):
        @pl.when(has(way, d))
        def _():
            for p in range(pieces):
                z_copy(way, d, p).wait_recv()
                if d < 8:
                    z_copy(way, d + 1, p).start()
                if d == 8 and (p + 1) % (pieces // 2) == 0:
                    q = (p + 1) // (pieces // 2) - 1
                    y_copy(1, q, 1, zb.at[way, d]).start()
                    y_copy(1, q, 3, zb.at[way, d]).start()
            if d < 8:
                delta = d if way == 0 else 8 - d

                @pl.when((delta <= i) & (rem(i + h + delta, 2) == 0))
                def _():
                    c_copy(way, zb.at[way, d], target(delta)).start()
            else:
                @pl.when(role == 0)
                def _():
                    c_copy(1, zb.at[way, d], target(0)).start()

    for way, d in ((0, 1), (1, 1), (0, 2), (1, 2), (0, 3), (1, 3)):
        take(way, d)
    y_relay(0, 0)
    y_relay(0, 1)
    p_copy(0).wait_recv()
    p_copy(1).start()
    for way, d in ((0, 4), (1, 4), (0, 5), (1, 5)):
        take(way, d)

    def weigh(where):
        both = ext[...] * ext[pl.ds(y, 1), :]
        own = pri[where * 2]
        tab[...] = both[:, 0:1] * own[0:1, :] + both[:, 1:2] * own[1:2, :]

    def scale(where, s, src):
        value = src.astype(jnp.float32) * tab[pl.ds(rem(y + 4 - s, 4), 1), :]
        high = value.astype(jnp.bfloat16)
        cut = pl.ds(s * rows, rows)
        sh[where, cut, :] = high
        sl[where, cut, :] = (value - high.astype(jnp.float32)).astype(jnp.bfloat16)

    for q in (0, 1):
        y_copy(0, q, 1 if q == 1 else 3, j_ref).wait_recv()
        y_copy(0, q, 2, j_ref).wait_recv()
    for load in loads[1:]:
        load.wait()
    weigh(0)
    scale(0, 0, zb[0, 0])
    for s in (1, 2, 3):
        scale(0, s, rb[s - 1, 0])
    for way, d in ((0, 6), (1, 6), (0, 7), (1, 7), (0, 8), (1, 8)):
        take(way, d)
    p_copy(1).wait_recv()
    weigh(1)
    scale(1, 0, zb[1 - kind, 8])

    def active(dx):
        return rem(x + dx, 4) * 2 + h <= i

    def columns(where, dx):
        j = rem(x + dx, 4) * 2 + h
        delta = i - j
        if where == 0:
            own = zb[0, delta]
        else:
            own = zb[jnp.where(delta == 0, 1 - kind, 1), 8 - delta]
        return jnp.concatenate([own, cb[dx, where]], axis=0)

    def half_product(where, cut, cols):
        return lax.dot_general(
            sh[where, cut, :], cols, NT, preferred_element_type=jnp.float32
        ) + lax.dot_general(sl[where, cut, :], cols, NT, preferred_element_type=jnp.float32)

    def block(s):
        return pl.ds(s * rows, rows)

    def a_copy(s):
        return send(
            part.at[2, block(s), :], ra.at[s], as_.at[s], ar.at[s],
            x_next if s % 2 == 0 else x_prev,
        )

    def x_copy(k, s):
        return send(
            part.at[1 if k == 0 else 3, block(s), :], rx.at[k, block(s), :],
            xs.at[k, s], xr.at[k, s], x_next if k == 0 else x_prev,
        )

    def compute(s):
        for dx in (2, 1, 3, 0):
            @pl.when(active(dx))
            def _():
                if s == 0:
                    c_copy(0, j_ref, dx).wait_recv()
                    c_copy(1, j_ref, dx).wait_recv()
                part[dx, block(s), :] = half_product(0, block(s), columns(0, dx)) + half_product(
                    1, block(s), columns(1, dx)
                )
                if dx == 2:
                    a_copy(s).start()
                if dx == 1 and s % 2 == 1:
                    x_copy(0, s).start()
                if dx == 3 and s % 2 == 0:
                    x_copy(1, s).start()

    def relay(s):
        dx = 1 if s % 2 == 0 else 3

        @pl.when(active(dx))
        def _():
            a_copy(s).wait_recv()
            part[dx, block(s), :] = part[dx, block(s), :] + ra[s]
            x_copy(s % 2, s).start()

    def f_copy(s):
        cut = pl.ds(s * rows, rows)
        device = y_prev if s == 1 else y_next
        return send(fin.at[cut, :], yb.at[s // 2], fs.at[s // 2], fr.at[s // 2], device)

    def g_copy(q, leg):
        src = fin.at[pl.ds(2 * rows + q * half_rows, half_rows), :] if leg == 0 else fb.at[q]
        dst = fb.at[q] if leg == 0 else yb.at[2, pl.ds(q * half_rows, half_rows), :]
        return send(src, dst, gs.at[leg, q], gr.at[leg, q], y_next if q == 0 else y_prev)

    j_own = x * 2 + h
    mine = j_own <= i

    def final(s):
        @pl.when(mine)
        def _():
            x_copy(0, s).wait_recv()
            x_copy(1, s).wait_recv()
            fin[block(s), :] = part[0, block(s), :] + rx[0, block(s), :] + rx[1, block(s), :]
            if s == 2:
                g_copy(0, 0).start()
                g_copy(1, 0).start()
            elif s > 0:
                f_copy(s).start()

    compute(0)
    y_relay(1, 0)
    y_relay(1, 1)
    y_copy(1, 1, 1, j_ref).wait_recv()
    scale(1, 1, rb[0, 1])
    compute(1)
    relay(0)
    for q in (0, 1):
        y_copy(1, q, 2, j_ref).wait_recv()
    scale(1, 2, rb[1, 1])
    compute(2)
    relay(1)
    y_copy(1, 0, 3, j_ref).wait_recv()
    scale(1, 3, rb[2, 1])
    compute(3)
    final(0)
    relay(2)
    final(1)
    relay(3)
    final(2)
    final(3)

    @pl.when(mine)
    def _():
        def place(s, value):
            source = rem(y + s, 4)
            row = ((i * 2 + c) * 4 + y) * rows + lax.broadcasted_iota(jnp.int32, (rows, rows), 0)
            lane = lax.broadcasted_iota(jnp.int32, (rows, rows), 1)
            for k in (0, 1):
                block = (c if k == 0 else 1 - c) * 4 + source
                col = j_own * (rows * 8) + block * rows + lane
                piece = value[:, k * rows:(k + 1) * rows]
                out_ref[:, pl.ds(pl.multiple_of(block * rows, rows), rows)] = jnp.where(
                    col <= row, piece, 0.0
                )

        place(0, fin[0:rows, :])
        for q in (0, 1):
            g_copy(q, 0).wait_recv()
            g_copy(q, 1).start()
        for s in (1, 3):
            f_copy(s).wait_recv()
            place(s, yb[s // 2])
        for q in (0, 1):
            g_copy(q, 1).wait_recv()
        place(2, yb[2])

    @pl.when(j_own > i)
    def _():
        out_ref[...] = jnp.zeros_like(out_ref)

    for k in (0, 1):
        p_copy(k).wait_send()
    for way in (0, 1):
        for d in range(1, 9):
            @pl.when(sends(way, d))
            def _():
                for p in range(pieces):
                    z_copy(way, d, p).wait_send()
    for where in (0, 1):
        for q in (0, 1):
            for s in (1, 2, 3):
                y_copy(where, q, s, j_ref).wait_send()
    for dx in range(4):
        @pl.when(active(dx))
        def _():
            for where in (0, 1):
                c_copy(where, j_ref, dx).wait_send()
            if dx == 2:
                for s in range(4):
                    a_copy(s).wait_send()
            if dx == 1 or dx == 3:
                for s in range(4):
                    x_copy(0 if dx == 1 else 1, s).wait_send()

    @pl.when(mine)
    def _():
        for s in (1, 3):
            f_copy(s).wait_send()
        for q in (0, 1):
            g_copy(q, 0).wait_send()
            g_copy(q, 1).wait_send()


def on_device(pieces, jacobian, extinction, prior_var):
    rows, vox = jacobian.shape
    width = rows * 8
    dma = pltpu.SemaphoreType.DMA
    vmem = pltpu.VMEM
    f32, bf16 = jnp.float32, jnp.bfloat16
    return pl.pallas_call(
        functools.partial(kernel, pieces),
        out_shape=jax.ShapeDtypeStruct((rows, width), f32),
        in_specs=[
            pl.BlockSpec(memory_space=pl.ANY),
            pl.BlockSpec(memory_space=pl.ANY),
            pl.BlockSpec(memory_space=pl.ANY),
        ],
        out_specs=pl.BlockSpec(memory_space=pltpu.VMEM),
        scratch_shapes=[
            vmem((2, 9, rows, vox), bf16),
            vmem((4, 2, rows, vox), bf16),
            vmem((3, 2, rows, vox), bf16),
            vmem((4, 2), f32),
            vmem((3, 2, vox), f32),
            vmem((4, vox), f32),
            vmem((2, rows * 4, vox), bf16),
            vmem((2, rows * 4, vox), bf16),
            vmem((4, rows * 4, rows * 2), f32),
            vmem((4, rows, rows * 2), f32),
            vmem((2, rows * 4, rows * 2), f32),
            vmem((rows * 4, rows * 2), f32),
            vmem((3, rows, rows * 2), f32),
            vmem((2, rows // 2, rows * 2), f32),
            dma((2, 9, pieces)), dma((2, 9, pieces)),
            dma((2, 4)), dma((2, 4)),
            dma((2, 2, 3)), dma((2, 2, 3)),
            dma((4,)), dma((4,)),
            dma((2, 4)), dma((2, 4)),
            dma((2,)), dma((2,)),
            dma((2, 2)), dma((2, 2)),
            dma((2,)), dma((2,)),
            dma((3,)),
        ],
        compiler_params=pltpu.CompilerParams(
            collective_id=0, has_side_effects=True, vmem_limit_bytes=67043328
        ),
    )(jacobian, extinction, prior_var)


def solution(mesh):
    return jax.shard_map(
        functools.partial(on_device, 4),
        mesh=mesh,
        in_specs=(P(("row", "wl"), "vox"), P(), P(None, "vox")),
        out_specs=P(("row", "wl"), "vox"),
        check_vma=False,
    )
```

```python
import functools
import jax
import jax.numpy as jnp
from jax import lax
from jax.experimental import pallas as pl
from jax.experimental.pallas import tpu as pltpu
from jax.sharding import PartitionSpec as P

MESH = pl.DeviceIdType.MESH
NT = (((1,), (1,)), ((), ()))


def rem(a, n):
    return lax.rem(a, jnp.int32(n))


def div(a, n):
    return lax.div(a, jnp.int32(n))


def kernel(
    pieces,
    j_ref, ext_ref, pri_ref, out_ref,
    zb, cb, rb, ext, pri, tab, sc, part, ra, rx, fin, yb,
    zs, zr, cs, cr, ys, yr, as_, ar, xs, xr, fs, fr, ps, pr, ls,
):
    rows, vox = j_ref.shape
    step = rows // pieces
    half_rows = rows // 2
    v = lax.axis_index("vox")
    r = lax.axis_index("row")
    y = lax.axis_index("wl")
    x, h = div(v, 2), rem(v, 2)
    i, c = div(r, 2), rem(r, 2)
    z = h * 8 + i
    role = rem(i + h, 2)
    kind = rem(i + h + div(i, 7) * c, 2)

    def at(x_=None, z_=None, y_=None, c_=None):
        x_ = x if x_ is None else x_
        z_ = z if z_ is None else z_
        y_ = y if y_ is None else y_
        c_ = c if c_ is None else c_
        return {"vox": x_ * 2 + div(z_, 8), "row": rem(z_, 8) * 2 + c_, "wl": y_}

    x_next, x_prev = at(x_=rem(x + 1, 4)), at(x_=rem(x + 3, 4))
    y_next, y_far, y_prev = (at(y_=rem(y + k, 4)) for k in (1, 2, 3))
    z_next, z_prev = at(z_=rem(z + 1, 16)), at(z_=rem(z + 15, 16))
    z_up, z_down = at(z_=rem(z + 4, 16)), at(z_=rem(z + 12, 16))
    other = at(c_=1 - c)

    barrier = pltpu.get_barrier_semaphore()
    partners = (z_up, z_down, z_next, z_prev, y_far, y_next, y_prev, x_next, x_prev, other)
    for device in partners:
        pl.semaphore_signal(barrier, inc=1, device_id=device, device_id_type=MESH)
    loads = [
        pltpu.make_async_copy(src, dst, ls.at[k])
        for k, (src, dst) in enumerate(((j_ref, zb.at[0, 0]), (ext_ref, ext), (pri_ref, pri.at[0])))
    ]
    for load in loads:
        load.start()
    loads[0].wait()
    pl.semaphore_wait(barrier, len(partners))

    def send(src, dst, ssem, rsem, device):
        return pltpu.make_async_remote_copy(
            src_ref=src, dst_ref=dst, send_sem=ssem, recv_sem=rsem,
            device_id=device, device_id_type=MESH,
        )

    def source(way, d):
        s = rem(z + 16 - d, 16) if way == 0 else rem(z + d, 16)
        place = rem(s, 8)
        return rem(div(s, 8) + place + div(place, 7) * c, 2)

    def has(way, d):
        return source(way, d) == way

    def sends(way, d):
        return source(way, d - 1) == way

    def z_copy(way, d, p):
        cut = pl.ds(p * step, step)
        src = zb.at[0, 0] if d == 1 else zb.at[way, d - 1]
        device = z_next if way == 0 else z_prev
        return send(
            src.at[cut, :], zb.at[way, d, cut, :], zs.at[way, d, p], zr.at[way, d, p], device
        )

    def target(delta):
        return div(i - delta - h, 2)

    def c_copy(where, src, t, q):
        cut = pl.ds(q * half_rows, half_rows)
        return send(
            src.at[cut, :], cb.at[t, where, cut, :], cs.at[where, t, q], cr.at[where, t, q], other
        )

    def y_copy(where, q, s, src):
        cut = pl.ds(q * half_rows, half_rows)
        return send(
            src.at[cut, :], rb.at[s - 1, where, cut, :],
            ys.at[where, q, s - 1], yr.at[where, q, s - 1],
            y_prev if s == 3 or (s == 2 and q == 1) else y_next,
        )

    def y_relay(where, q):
        s = 1 if q == 0 else 3
        y_copy(where, q, s, rb.at[s - 1, where]).wait_recv()
        y_copy(where, q, 2, rb.at[s - 1, where]).start()

    def p_copy(k):
        return send(pri_ref if k == 0 else pri.at[1], pri.at[k + 1], ps.at[k], pr.at[k], z_up)

    def start_z(way, d, p):
        @pl.when(sends(way, d))
        def _():
            z_copy(way, d, p).start()

    for p in range(pieces):
        start_z(0, 1, p)
        start_z(1, 1, p)
    p_copy(0).start()
    for q in (0, 1):
        for s in (1, 3):
            y_copy(0, q, s, zb.at[0, 0]).start()

    @pl.when(role == 0)
    def _():
        for q in (0, 1):
            c_copy(0, zb.at[0, 0], target(0), q).start()

    def take(d):
        for p in range(pieces):
            for way in (0, 1):
                @pl.when(has(way, d))
                def _():
                    z_copy(way, d, p).wait_recv()
                    if d < 8:
                        z_copy(way, d + 1, p).start()
                    if (p + 1) % (pieces // 2) != 0:
                        return
                    q = (p + 1) // (pieces // 2) - 1
                    chunk = zb.at[way, d]
                    if d < 8:
                        delta = d if way == 0 else 8 - d

                        @pl.when((delta <= i) & (rem(i + h + delta, 2) == 0))
                        def _():
                            c_copy(way, chunk, target(delta), q).start()
                    else:
                        y_copy(1, q, 1, chunk).start()
                        y_copy(1, q, 3, chunk).start()

                        @pl.when(role == 0)
                        def _():
                            c_copy(1, chunk, target(0), q).start()

    for d in (1, 2, 3):
        take(d)
    y_relay(0, 0)
    y_relay(0, 1)
    p_copy(0).wait_recv()
    p_copy(1).start()
    for d in (4, 5):
        take(d)

    def weigh(where):
        lane = lax.broadcasted_iota(jnp.int32, (2, 4), 1)
        values = ext[...]
        both = values * jnp.sum(jnp.where(lane == y, values, 0.0), axis=1, keepdims=True)
        own = pri[where * 2]
        for a in range(4):
            tab[a:a + 1, :] = both[0:1, a:a + 1] * own[0:1, :] + both[1:2, a:a + 1] * own[1:2, :]

    def scale(where, s, src, high_at, low_at):
        value = src.astype(jnp.float32) * tab[pl.ds(rem(y + 4 - s, 4), 1), :]
        high = value.astype(jnp.bfloat16)
        count = src.shape[0]
        sc[where, high_at:high_at + count, :] = high
        sc[where, low_at:low_at + count, :] = (value - high.astype(jnp.float32)).astype(jnp.bfloat16)

    def scale_own(s, src):
        scale(0, s, src, s * rows, (4 + s) * rows)

    def scale_far(b, src):
        scale(1, b // 2, src, b * rows, b * rows + half_rows)

    def active(t):
        return t * 2 + h <= i

    def columns(where, t):
        delta = i - t * 2 - h
        if where == 0:
            own = zb[0, delta]
        else:
            own = zb[jnp.where(delta == 0, 1 - kind, 1), 8 - delta]
        return jnp.concatenate([own, cb[t, where]], axis=0)

    def block(b):
        return pl.ds(b * half_rows, half_rows)

    far_x = rem(x + 2, 4)
    sides = (rem(x + 1, 4), rem(x + 3, 4))

    def a_copy(b):
        return send(
            part.at[far_x, block(b), :], ra.at[b], as_.at[b], ar.at[b],
            x_next if b % 2 == 0 else x_prev,
        )

    def x_copy(k, b):
        return send(
            part.at[sides[k], block(b), :], rx.at[k, block(b), :],
            xs.at[k, b], xr.at[k, b], x_next if k == 0 else x_prev,
        )

    def own_half():
        for t in range(4):
            @pl.when(active(t))
            def _():
                for q in (0, 1):
                    c_copy(0, j_ref, t, q).wait_recv()
                both = lax.dot_general(
                    sc[0], columns(0, t), NT, preferred_element_type=jnp.float32
                )
                part[t] = both[:rows * 4] + both[rows * 4:]

    def compute(b):
        for t in range(4):
            @pl.when(active(t))
            def _():
                if b == 0:
                    for q in (0, 1):
                        c_copy(1, j_ref, t, q).wait_recv()
                both = lax.dot_general(
                    sc[1, b * rows:(b + 1) * rows, :], columns(1, t), NT,
                    preferred_element_type=jnp.float32,
                )
                part[t, block(b), :] = part[t, block(b), :] + (both[:half_rows] + both[half_rows:])

                @pl.when(far_x == t)
                def _():
                    a_copy(b).start()

                @pl.when(sides[1 - b % 2] == t)
                def _():
                    x_copy(1 - b % 2, b).start()

    def relay(b):
        k = b % 2

        @pl.when(active(sides[k]))
        def _():
            a_copy(b).wait_recv()
            part[sides[k], block(b), :] = part[sides[k], block(b), :] + ra[b]
            x_copy(k, b).start()

    def f_copy(b):
        device = (None, y_prev, y_far, y_next)[b // 2]
        return send(fin.at[block(b), :], yb.at[block(b), :], fs.at[b], fr.at[b], device)

    j_own = x * 2 + h
    mine = j_own <= i

    def final(b):
        @pl.when(mine)
        def _():
            x_copy(0, b).wait_recv()
            x_copy(1, b).wait_recv()
            fin[block(b), :] = part[x, block(b), :] + rx[0, block(b), :] + rx[1, block(b), :]
            if b // 2 != 0:
                f_copy(b).start()

    for q in (0, 1):
        y_copy(0, q, 1 if q == 1 else 3, j_ref).wait_recv()
        y_copy(0, q, 2, j_ref).wait_recv()
    for load in loads[1:]:
        load.wait()
    weigh(0)
    scale_own(0, zb[0, 0])
    for s in (1, 2, 3):
        scale_own(s, rb[s - 1, 0])
    for d in (6, 7):
        take(d)
    own_half()
    p_copy(1).wait_recv()
    weigh(1)

    take(8)

    def arrived(b):
        s, q = b // 2, b % 2
        if s == 0:
            src = zb[1 - kind, 8, q * half_rows:(q + 1) * half_rows, :]
        else:
            src = rb[s - 1, 1, q * half_rows:(q + 1) * half_rows, :]
        scale_far(b, src)
        compute(b)

    arrived(0)
    arrived(1)
    y_relay(1, 0)
    arrived(2)
    y_relay(1, 1)
    arrived(7)
    y_copy(1, 1, 1, j_ref).wait_recv()
    arrived(3)
    relay(0)
    relay(1)
    y_copy(1, 0, 3, j_ref).wait_recv()
    arrived(6)
    y_copy(1, 0, 2, j_ref).wait_recv()
    arrived(4)
    y_copy(1, 1, 2, j_ref).wait_recv()
    arrived(5)
    relay(2)
    relay(7)
    relay(3)
    relay(6)
    final(0)
    final(1)
    final(2)
    final(7)
    relay(4)
    relay(5)
    final(3)
    final(6)
    final(4)
    final(5)

    @pl.when(mine)
    def _():
        def place(s, value):
            source = rem(y + s, 4)
            row = ((i * 2 + c) * 4 + y) * rows + lax.broadcasted_iota(jnp.int32, (rows, rows), 0)
            lane = lax.broadcasted_iota(jnp.int32, (rows, rows), 1)
            for k in (0, 1):
                block = (c if k == 0 else 1 - c) * 4 + source
                col = j_own * (rows * 8) + block * rows + lane
                piece = value[:, k * rows:(k + 1) * rows]
                out_ref[:, pl.ds(pl.multiple_of(block * rows, rows), rows)] = jnp.where(
                    col <= row, piece, 0.0
                )

        place(0, fin[0:rows, :])
        for s in (1, 3, 2):
            for q in (0, 1):
                f_copy(s * 2 + q).wait_recv()
            place(s, yb[s * rows:(s + 1) * rows, :])

    @pl.when(j_own > i)
    def _():
        out_ref[...] = jnp.zeros_like(out_ref)

    for k in (0, 1):
        p_copy(k).wait_send()
    for way in (0, 1):
        for d in range(1, 9):
            @pl.when(sends(way, d))
            def _():
                for p in range(pieces):
                    z_copy(way, d, p).wait_send()
    for where in (0, 1):
        for q in (0, 1):
            for s in (1, 2, 3):
                y_copy(where, q, s, j_ref).wait_send()
    for t in range(4):
        @pl.when(active(t))
        def _():
            for where in (0, 1):
                for q in (0, 1):
                    c_copy(where, j_ref, t, q).wait_send()

    @pl.when(active(far_x))
    def _():
        for b in range(8):
            a_copy(b).wait_send()
    for k in (0, 1):
        @pl.when(active(sides[k]))
        def _():
            for b in range(8):
                x_copy(k, b).wait_send()

    @pl.when(mine)
    def _():
        for b in range(2, 8):
            f_copy(b).wait_send()


def on_device(pieces, jacobian, extinction, prior_var):
    rows, vox = jacobian.shape
    width = rows * 8
    dma = pltpu.SemaphoreType.DMA
    vmem = pltpu.VMEM
    f32, bf16 = jnp.float32, jnp.bfloat16
    return pl.pallas_call(
        functools.partial(kernel, pieces),
        out_shape=jax.ShapeDtypeStruct((rows, width), f32),
        in_specs=[
            pl.BlockSpec(memory_space=pl.ANY),
            pl.BlockSpec(memory_space=pl.ANY),
            pl.BlockSpec(memory_space=pl.ANY),
        ],
        out_specs=pl.BlockSpec(memory_space=pltpu.VMEM),
        scratch_shapes=[
            vmem((2, 9, rows, vox), bf16),
            vmem((4, 2, rows, vox), bf16),
            vmem((3, 2, rows, vox), bf16),
            vmem((2, 4), f32),
            vmem((3, 2, vox), f32),
            vmem((4, vox), f32),
            vmem((2, rows * 8, vox), bf16),
            vmem((4, rows * 4, rows * 2), f32),
            vmem((8, rows // 2, rows * 2), f32),
            vmem((2, rows * 4, rows * 2), f32),
            vmem((rows * 4, rows * 2), f32),
            vmem((rows * 4, rows * 2), f32),
            dma((2, 9, pieces)), dma((2, 9, pieces)),
            dma((2, 4, 2)), dma((2, 4, 2)),
            dma((2, 2, 3)), dma((2, 2, 3)),
            dma((8,)), dma((8,)),
            dma((2, 8)), dma((2, 8)),
            dma((8,)), dma((8,)),
            dma((2,)), dma((2,)),
            dma((3,)),
        ],
        compiler_params=pltpu.CompilerParams(
            collective_id=0, has_side_effects=True, vmem_limit_bytes=67043328
        ),
    )(jacobian, extinction.T, prior_var)


def solution(mesh):
    return jax.shard_map(
        functools.partial(on_device, 4),
        mesh=mesh,
        in_specs=(P(("row", "wl"), "vox"), P(), P(None, "vox")),
        out_specs=P(("row", "wl"), "vox"),
        check_vma=False,
    )
```

```python
import functools
import jax
import jax.numpy as jnp
from jax import lax
from jax.experimental import pallas as pl
from jax.experimental.pallas import tpu as pltpu
from jax.sharding import PartitionSpec as P

MESH = pl.DeviceIdType.MESH
NT = (((1,), (1,)), ((), ()))


def rem(a, n):
    return lax.rem(a, jnp.int32(n))


def div(a, n):
    return lax.div(a, jnp.int32(n))


def kernel(
    pieces,
    j_ref, ext_ref, pri_ref, out_ref,
    zb, rb, ext, pri, tab, sc, part, ra, rx, fin, yb,
    zs, zr, cs, cr, es, er, ys, yr, as_, ar, xs, xr, fs, fr, ps, pr, ls,
):
    rows, vox = j_ref.shape
    step = rows // pieces
    half_rows = rows // 2
    v = lax.axis_index("vox")
    r = lax.axis_index("row")
    y = lax.axis_index("wl")
    x, h = div(v, 2), rem(v, 2)
    i, c = div(r, 2), rem(r, 2)
    z = h * 8 + i
    role = rem(i + h, 2)
    kind = rem(i + h + div(i, 7) * c, 2)
    kind_other = rem(i + h + div(i, 7) * (1 - c), 2)

    def at(x_=None, z_=None, y_=None, c_=None):
        x_ = x if x_ is None else x_
        z_ = z if z_ is None else z_
        y_ = y if y_ is None else y_
        c_ = c if c_ is None else c_
        return {"vox": x_ * 2 + div(z_, 8), "row": rem(z_, 8) * 2 + c_, "wl": y_}

    x_next, x_prev = at(x_=rem(x + 1, 4)), at(x_=rem(x + 3, 4))
    y_next, y_far, y_prev = (at(y_=rem(y + k, 4)) for k in (1, 2, 3))
    z_next, z_prev = at(z_=rem(z + 1, 16)), at(z_=rem(z + 15, 16))
    z_up, z_down = at(z_=rem(z + 4, 16)), at(z_=rem(z + 12, 16))
    other = at(c_=1 - c)

    barrier = pltpu.get_barrier_semaphore()
    partners = (z_up, z_down, z_next, z_prev, y_far, y_next, y_prev, x_next, x_prev, other)
    for device in partners:
        pl.semaphore_signal(barrier, inc=1, device_id=device, device_id_type=MESH)
    loads = [
        pltpu.make_async_copy(src, dst, ls.at[k])
        for k, (src, dst) in enumerate(((j_ref, zb.at[c, 0, 0]), (ext_ref, ext), (pri_ref, pri.at[0])))
    ]
    for load in loads:
        load.start()
    loads[0].wait()
    pl.semaphore_wait(barrier, len(partners))

    def send(src, dst, ssem, rsem, device):
        return pltpu.make_async_remote_copy(
            src_ref=src, dst_ref=dst, send_sem=ssem, recv_sem=rsem,
            device_id=device, device_id_type=MESH,
        )

    def source(k, way, d):
        s = rem(z + 16 - d, 16) if way == 0 else rem(z + d, 16)
        place = rem(s, 8)
        return rem(div(s, 8) + place + (div(place, 7) if k else 0), 2)

    def has(k, way, d):
        return source(k, way, d) == way

    def sends(k, way, d):
        return source(k, way, d - 1) == way

    def z_copy(k, way, d, p):
        cut = pl.ds(p * step, step)
        src = zb.at[k, 0, 0] if d == 1 else zb.at[k, way, d - 1]
        device = z_next if way == 0 else z_prev
        return send(
            src.at[cut, :], zb.at[k, way, d, cut, :], zs.at[k, way, d, p], zr.at[k, way, d, p], device
        )

    def c_copy(k, way, d, q):
        cut = pl.ds(q * half_rows, half_rows)
        place = zb.at[k, way, d, cut, :]
        return send(place, place, cs.at[k, way, d, q], cr.at[k, way, d, q], other)

    def column_at(delta, way):
        return (delta >= 0) & (delta <= i) & (rem(i + h + delta, 2) == 0)

    def handed(k, way, d):
        if d == 8:
            return has(k, way, d) if k == 0 else has(k, way, d) & (role == 0)
        return has(k, way, d) & column_at(d if way == 0 else 8 - d, way)

    def e_copy():
        return send(zb.at[c, 0, 0], zb.at[c, 0, 0], es, er, other)

    first, second = c == 0, c == 1

    def y_copy(where, q, s, src):
        cut = pl.ds(q * half_rows, half_rows)
        return send(
            src.at[cut, :], rb.at[s - 1, where, cut, :],
            ys.at[where, q, s - 1], yr.at[where, q, s - 1],
            y_prev if s == 3 or (s == 2 and q == 1) else y_next,
        )

    def y_relay(where, q):
        s = 1 if q == 0 else 3
        y_copy(where, q, s, rb.at[s - 1, where]).wait_recv()
        y_copy(where, q, 2, rb.at[s - 1, where]).start()

    def p_copy(k):
        return send(pri_ref if k == 0 else pri.at[1], pri.at[k + 1], ps.at[k], pr.at[k], z_up)

    e_copy().start()

    def start_z(k):
        for p in range(pieces):
            for way in (0, 1):
                @pl.when(second & sends(k, way, 1))
                def _():
                    z_copy(k, way, 1, p).start()

    start_z(1)
    p_copy(0).start()
    for q in (0, 1):
        for s in (1, 3):
            y_copy(0, q, s, zb.at[c, 0, 0]).start()

    e_copy().wait_recv()
    start_z(0)

    def y_start(src, q):
        y_copy(1, q, 1, src).start()
        y_copy(1, q, 3, src).start()

    def take(d):
        def move(k, way, p):
            z_copy(k, way, d, p).wait_recv()
            if d < 8:
                z_copy(k, way, d + 1, p).start()
            if (p + 1) % (pieces // 2) != 0:
                return
            q = (p + 1) // (pieces // 2) - 1
            if d == 8 and k == 1:
                y_start(zb.at[k, way, d], q)

            @pl.when(handed(k, way, d))
            def _():
                c_copy(k, way, d, q).start()

        for p in range(pieces):
            for k in (1, 0):
                for way in (0, 1):
                    pl.when(second & has(k, way, d))(functools.partial(move, k, way, p))

    for d in (1, 2, 3):
        take(d)
    y_relay(0, 0)
    y_relay(0, 1)
    p_copy(0).wait_recv()
    p_copy(1).start()
    for d in (4, 5):
        take(d)

    def weigh(where):
        lane = lax.broadcasted_iota(jnp.int32, (2, 4), 1)
        values = ext[...]
        both = values * jnp.sum(jnp.where(lane == y, values, 0.0), axis=1, keepdims=True)
        own = pri[where * 2]
        for a in range(4):
            tab[a:a + 1, :] = both[0:1, a:a + 1] * own[0:1, :] + both[1:2, a:a + 1] * own[1:2, :]

    def scale(where, s, src, high_at, low_at):
        value = src.astype(jnp.float32) * tab[pl.ds(rem(y + 4 - s, 4), 1), :]
        high = value.astype(jnp.bfloat16)
        count = src.shape[0]
        sc[where, high_at:high_at + count, :] = high
        sc[where, low_at:low_at + count, :] = (value - high.astype(jnp.float32)).astype(jnp.bfloat16)

    def scale_own(s, src):
        scale(0, s, src, s * rows, (4 + s) * rows)

    def scale_far(b, src):
        scale(1, b // 2, src, b * rows, b * rows + half_rows)

    def active(t):
        return t * 2 + h <= i

    def columns(where, t):
        delta = i - t * 2 - h
        if where == 0:
            pair = zb[c, 0, delta], zb[1 - c, 0, delta]
        else:
            at_end = delta == 0
            pair = (
                zb[c, jnp.where(at_end, 1 - kind, 1), 8 - delta],
                zb[1 - c, jnp.where(at_end, 1 - kind_other, 1), 8 - delta],
            )
        return jnp.concatenate(pair, axis=0)

    def taken(where, t):
        delta = i - t * 2 - h
        for k in (0, 1):
            for q in (0, 1):
                if where == 0:
                    @pl.when(first & (delta > 0))
                    def _():
                        c_copy(k, 0, delta, q).wait_recv()
                else:
                    @pl.when(first & (delta > 0))
                    def _():
                        c_copy(k, 1, 8 - delta, q).wait_recv()
        if where == 1:
            @pl.when(first & (delta == 0))
            def _():
                for q in (0, 1):
                    c_copy(1, 1 - kind_other, 8, q).wait_recv()

    def block(b):
        return pl.ds(b * half_rows, half_rows)

    far_x = rem(x + 2, 4)
    sides = (rem(x + 1, 4), rem(x + 3, 4))

    def a_copy(b):
        return send(
            part.at[far_x, block(b), :], ra.at[b], as_.at[b], ar.at[b],
            x_next if b % 2 == 0 else x_prev,
        )

    def x_copy(k, b):
        return send(
            part.at[sides[k], block(b), :], rx.at[k, block(b), :],
            xs.at[k, b], xr.at[k, b], x_next if k == 0 else x_prev,
        )

    def own_half():
        for t in range(4):
            @pl.when(active(t))
            def _():
                taken(0, t)
                both = lax.dot_general(
                    sc[0], columns(0, t), NT, preferred_element_type=jnp.float32
                )
                part[t] = both[:rows * 4] + both[rows * 4:]

    def compute(b):
        for t in range(4):
            @pl.when(active(t))
            def _():
                if b == 0:
                    taken(1, t)
                both = lax.dot_general(
                    sc[1, b * rows:(b + 1) * rows, :], columns(1, t), NT,
                    preferred_element_type=jnp.float32,
                )
                part[t, block(b), :] = part[t, block(b), :] + (both[:half_rows] + both[half_rows:])

                @pl.when(far_x == t)
                def _():
                    a_copy(b).start()

                @pl.when(sides[1 - b % 2] == t)
                def _():
                    x_copy(1 - b % 2, b).start()

    def relay(b):
        k = b % 2

        @pl.when(active(sides[k]))
        def _():
            a_copy(b).wait_recv()
            part[sides[k], block(b), :] = part[sides[k], block(b), :] + ra[b]
            x_copy(k, b).start()

    def f_copy(b):
        device = (None, y_prev, y_far, y_next)[b // 2]
        return send(fin.at[block(b), :], yb.at[block(b), :], fs.at[b], fr.at[b], device)

    j_own = x * 2 + h
    mine = j_own <= i

    def final(b):
        @pl.when(mine)
        def _():
            x_copy(0, b).wait_recv()
            x_copy(1, b).wait_recv()
            fin[block(b), :] = part[x, block(b), :] + rx[0, block(b), :] + rx[1, block(b), :]
            if b // 2 != 0:
                f_copy(b).start()

    for q in (0, 1):
        y_copy(0, q, 1 if q == 1 else 3, j_ref).wait_recv()
        y_copy(0, q, 2, j_ref).wait_recv()
    for load in loads[1:]:
        load.wait()
    weigh(0)
    scale_own(0, zb[c, 0, 0])
    for s in (1, 2, 3):
        scale_own(s, rb[s - 1, 0])
    for d in (6, 7):
        take(d)
    own_half()
    p_copy(1).wait_recv()
    weigh(1)

    take(8)
    for q in (0, 1):
        @pl.when(first)
        def _():
            c_copy(0, 1 - kind, 8, q).wait_recv()
            y_start(zb.at[0, 1 - kind, 8], q)

    def arrived(b):
        s, q = b // 2, b % 2
        if s == 0:
            src = zb[c, 1 - kind, 8, q * half_rows:(q + 1) * half_rows, :]
        else:
            src = rb[s - 1, 1, q * half_rows:(q + 1) * half_rows, :]
        scale_far(b, src)
        compute(b)

    arrived(0)
    arrived(1)
    y_relay(1, 0)
    arrived(2)
    y_relay(1, 1)
    arrived(7)
    y_copy(1, 1, 1, j_ref).wait_recv()
    arrived(3)
    relay(0)
    relay(1)
    y_copy(1, 0, 3, j_ref).wait_recv()
    arrived(6)
    y_copy(1, 0, 2, j_ref).wait_recv()
    arrived(4)
    y_copy(1, 1, 2, j_ref).wait_recv()
    arrived(5)
    relay(2)
    relay(7)
    relay(3)
    relay(6)
    final(0)
    final(1)
    final(2)
    final(7)
    relay(4)
    relay(5)
    final(3)
    final(6)
    final(4)
    final(5)

    @pl.when(mine)
    def _():
        def place(s, value):
            source = rem(y + s, 4)
            row = ((i * 2 + c) * 4 + y) * rows + lax.broadcasted_iota(jnp.int32, (rows, rows), 0)
            lane = lax.broadcasted_iota(jnp.int32, (rows, rows), 1)
            for k in (0, 1):
                block = (c if k == 0 else 1 - c) * 4 + source
                col = j_own * (rows * 8) + block * rows + lane
                piece = value[:, k * rows:(k + 1) * rows]
                out_ref[:, pl.ds(pl.multiple_of(block * rows, rows), rows)] = jnp.where(
                    col <= row, piece, 0.0
                )

        place(0, fin[0:rows, :])
        for s in (1, 3, 2):
            for q in (0, 1):
                f_copy(s * 2 + q).wait_recv()
            place(s, yb[s * rows:(s + 1) * rows, :])

    @pl.when(j_own > i)
    def _():
        out_ref[...] = jnp.zeros_like(out_ref)

    for k in (0, 1):
        p_copy(k).wait_send()
    e_copy().wait_send()
    for k in (0, 1):
        for way in (0, 1):
            for d in range(1, 9):
                @pl.when(second & sends(k, way, d))
                def _():
                    for p in range(pieces):
                        z_copy(k, way, d, p).wait_send()

                @pl.when(second & handed(k, way, d))
                def _():
                    for q in (0, 1):
                        c_copy(k, way, d, q).wait_send()
    for where in (0, 1):
        for q in (0, 1):
            for s in (1, 2, 3):
                y_copy(where, q, s, j_ref).wait_send()
    @pl.when(active(far_x))
    def _():
        for b in range(8):
            a_copy(b).wait_send()
    for k in (0, 1):
        @pl.when(active(sides[k]))
        def _():
            for b in range(8):
                x_copy(k, b).wait_send()

    @pl.when(mine)
    def _():
        for b in range(2, 8):
            f_copy(b).wait_send()


def on_device(pieces, jacobian, extinction, prior_var):
    rows, vox = jacobian.shape
    width = rows * 8
    dma = pltpu.SemaphoreType.DMA
    vmem = pltpu.VMEM
    f32, bf16 = jnp.float32, jnp.bfloat16
    return pl.pallas_call(
        functools.partial(kernel, pieces),
        out_shape=jax.ShapeDtypeStruct((rows, width), f32),
        in_specs=[
            pl.BlockSpec(memory_space=pl.ANY),
            pl.BlockSpec(memory_space=pl.ANY),
            pl.BlockSpec(memory_space=pl.ANY),
        ],
        out_specs=pl.BlockSpec(memory_space=pltpu.VMEM),
        scratch_shapes=[
            vmem((2, 2, 9, rows, vox), bf16),
            vmem((3, 2, rows, vox), bf16),
            vmem((2, 4), f32),
            vmem((3, 2, vox), f32),
            vmem((4, vox), f32),
            vmem((2, rows * 8, vox), bf16),
            vmem((4, rows * 4, rows * 2), f32),
            vmem((8, rows // 2, rows * 2), f32),
            vmem((2, rows * 4, rows * 2), f32),
            vmem((rows * 4, rows * 2), f32),
            vmem((rows * 4, rows * 2), f32),
            dma((2, 2, 9, pieces)), dma((2, 2, 9, pieces)),
            dma((2, 2, 9, 2)), dma((2, 2, 9, 2)),
            dma, dma,
            dma((2, 2, 3)), dma((2, 2, 3)),
            dma((8,)), dma((8,)),
            dma((2, 8)), dma((2, 8)),
            dma((8,)), dma((8,)),
            dma((2,)), dma((2,)),
            dma((3,)),
        ],
        compiler_params=pltpu.CompilerParams(
            collective_id=0, has_side_effects=True, vmem_limit_bytes=67043328
        ),
    )(jacobian, extinction.T, prior_var)


def solution(mesh):
    return jax.shard_map(
        functools.partial(on_device, 4),
        mesh=mesh,
        in_specs=(P(("row", "wl"), "vox"), P(), P(None, "vox")),
        out_specs=P(("row", "wl"), "vox"),
        check_vma=False,
    )
```

```python
import functools
import jax
import jax.numpy as jnp
from jax import lax
from jax.experimental import pallas as pl
from jax.experimental.pallas import tpu as pltpu
from jax.sharding import PartitionSpec as P

MESH = pl.DeviceIdType.MESH
NT = (((1,), (1,)), ((), ()))


def rem(a, n):
    return lax.rem(a, jnp.int32(n))


def div(a, n):
    return lax.div(a, jnp.int32(n))


def kernel(
    pieces,
    j_ref, ext_ref, pri_ref, out_ref,
    zb, rb, ext, pri, tab, sc, part, ra, rx, fin, yb,
    zs, zr, cs, cr, es, er, ys, yr, as_, ar, xs, xr, fs, fr, ps, pr, ls,
):
    rows, vox = j_ref.shape
    step = rows // pieces
    half_rows = rows // 2
    v = lax.axis_index("vox")
    r = lax.axis_index("row")
    y = lax.axis_index("wl")
    x, h = div(v, 2), rem(v, 2)
    i, c = div(r, 2), rem(r, 2)
    z = h * 8 + i
    role = rem(i + h, 2)
    kind = rem(i + h + div(i, 7) * c, 2)
    kind_other = rem(i + h + div(i, 7) * (1 - c), 2)

    def at(x_=None, z_=None, y_=None, c_=None):
        x_ = x if x_ is None else x_
        z_ = z if z_ is None else z_
        y_ = y if y_ is None else y_
        c_ = c if c_ is None else c_
        return {"vox": x_ * 2 + div(z_, 8), "row": rem(z_, 8) * 2 + c_, "wl": y_}

    x_next, x_prev = at(x_=rem(x + 1, 4)), at(x_=rem(x + 3, 4))
    y_next, y_far, y_prev = (at(y_=rem(y + k, 4)) for k in (1, 2, 3))
    z_next, z_prev = at(z_=rem(z + 1, 16)), at(z_=rem(z + 15, 16))
    z_up, z_down = at(z_=rem(z + 4, 16)), at(z_=rem(z + 12, 16))
    other = at(c_=1 - c)

    barrier = pltpu.get_barrier_semaphore()
    partners = (z_up, z_down, z_next, z_prev, y_far, y_next, y_prev, x_next, x_prev, other)
    for device in partners:
        pl.semaphore_signal(barrier, inc=1, device_id=device, device_id_type=MESH)
    loads = [
        pltpu.make_async_copy(src, dst, ls.at[k])
        for k, (src, dst) in enumerate(((j_ref, zb.at[c, 0, 0]), (ext_ref, ext), (pri_ref, pri.at[0])))
    ]
    for load in loads:
        load.start()
    loads[0].wait()
    pl.semaphore_wait(barrier, len(partners))

    def send(src, dst, ssem, rsem, device):
        return pltpu.make_async_remote_copy(
            src_ref=src, dst_ref=dst, send_sem=ssem, recv_sem=rsem,
            device_id=device, device_id_type=MESH,
        )

    def source(k, way, d):
        s = rem(z + 16 - d, 16) if way == 0 else rem(z + d, 16)
        place = rem(s, 8)
        return rem(div(s, 8) + place + (div(place, 7) if k else 0), 2)

    def has(k, way, d):
        return source(k, way, d) == way

    def sends(k, way, d):
        return source(k, way, d - 1) == way

    def z_copy(k, way, d, p):
        cut = pl.ds(p * step, step)
        src = zb.at[k, 0, 0] if d == 1 else zb.at[k, way, d - 1]
        device = z_next if way == 0 else z_prev
        return send(
            src.at[cut, :], zb.at[k, way, d, cut, :], zs.at[k, way, d, p], zr.at[k, way, d, p], device
        )

    def c_copy(k, way, d, q):
        cut = pl.ds(q * half_rows, half_rows)
        place = zb.at[k, way, d, cut, :]
        return send(place, place, cs.at[k, way, d, q], cr.at[k, way, d, q], other)

    def column_at(delta, way):
        return (delta >= 0) & (delta <= i) & (rem(i + h + delta, 2) == 0)

    def handed(k, way, d):
        if d == 8:
            return has(k, way, d) if k == 0 else has(k, way, d) & (role == 0)
        return has(k, way, d) & column_at(d if way == 0 else 8 - d, way)

    def e_copy():
        return send(zb.at[c, 0, 0], zb.at[c, 0, 0], es, er, other)

    first, second = c == 0, c == 1

    def y_copy(where, q, s, src):
        cut = pl.ds(q * half_rows, half_rows)
        return send(
            src.at[cut, :], rb.at[s - 1, where, cut, :],
            ys.at[where, q, s - 1], yr.at[where, q, s - 1],
            y_prev if s == 3 or (s == 2 and q == 1) else y_next,
        )

    def y_relay(where, q):
        s = 1 if q == 0 else 3
        y_copy(where, q, s, rb.at[s - 1, where]).wait_recv()
        y_copy(where, q, 2, rb.at[s - 1, where]).start()

    def p_copy(k):
        return send(pri_ref if k == 0 else pri.at[1], pri.at[k + 1], ps.at[k], pr.at[k], z_up)

    e_copy().start()

    def start_z(k):
        for p in range(pieces):
            for way in (0, 1):
                @pl.when(second & sends(k, way, 1))
                def _():
                    z_copy(k, way, 1, p).start()

    start_z(1)
    p_copy(0).start()
    for q in (0, 1):
        for s in (1, 3):
            y_copy(0, q, s, zb.at[c, 0, 0]).start()

    e_copy().wait_recv()
    start_z(0)

    def y_start(src, q):
        y_copy(1, q, 1, src).start()
        y_copy(1, q, 3, src).start()

    def take(d):
        def move(k, way, p):
            z_copy(k, way, d, p).wait_recv()
            if d < 8:
                z_copy(k, way, d + 1, p).start()
            if (p + 1) % (pieces // 2) != 0:
                return
            q = (p + 1) // (pieces // 2) - 1
            if d == 8 and k == 1:
                y_start(zb.at[k, way, d], q)

            @pl.when(handed(k, way, d))
            def _():
                c_copy(k, way, d, q).start()

        for p in range(pieces):
            for k in (1, 0):
                for way in (0, 1):
                    pl.when(second & has(k, way, d))(functools.partial(move, k, way, p))

    for d in (1, 2, 3):
        take(d)
    y_relay(0, 0)
    y_relay(0, 1)
    p_copy(0).wait_recv()
    p_copy(1).start()
    for d in (4, 5):
        take(d)

    def weigh(where):
        lane = lax.broadcasted_iota(jnp.int32, (2, 4), 1)
        values = ext[...]
        both = values * jnp.sum(jnp.where(lane == y, values, 0.0), axis=1, keepdims=True)
        own = pri[where * 2]
        for a in range(4):
            tab[a:a + 1, :] = both[0:1, a:a + 1] * own[0:1, :] + both[1:2, a:a + 1] * own[1:2, :]

    def scale(where, s, src, high_at, low_at):
        value = src.astype(jnp.float32) * tab[pl.ds(rem(y + 4 - s, 4), 1), :]
        high = value.astype(jnp.bfloat16)
        count = src.shape[0]
        sc[where, high_at:high_at + count, :] = high
        sc[where, low_at:low_at + count, :] = (value - high.astype(jnp.float32)).astype(jnp.bfloat16)

    def scale_own(s, src):
        scale(0, s, src, s * rows, (4 + s) * rows)

    def scale_far(b, src):
        scale(1, b // 2, src, b * rows, b * rows + half_rows)

    def active(t):
        return t * 2 + h <= i

    def columns(where, t):
        delta = i - t * 2 - h
        if where == 0:
            pair = zb[c, 0, delta], zb[1 - c, 0, delta]
        else:
            at_end = delta == 0
            pair = (
                zb[c, jnp.where(at_end, 1 - kind, 1), 8 - delta],
                zb[1 - c, jnp.where(at_end, 1 - kind_other, 1), 8 - delta],
            )
        return jnp.concatenate(pair, axis=0)

    def taken(where, t):
        delta = i - t * 2 - h
        for k in (0, 1):
            for q in (0, 1):
                if where == 0:
                    @pl.when(first & (delta > 0))
                    def _():
                        c_copy(k, 0, delta, q).wait_recv()
                else:
                    @pl.when(first & (delta > 0))
                    def _():
                        c_copy(k, 1, 8 - delta, q).wait_recv()
        if where == 1:
            @pl.when(first & (delta == 0))
            def _():
                for q in (0, 1):
                    c_copy(1, 1 - kind_other, 8, q).wait_recv()

    def block(b):
        return pl.ds(b * half_rows, half_rows)

    far_x = rem(x + 2, 4)
    sides = (rem(x + 1, 4), rem(x + 3, 4))

    def a_copy(b):
        return send(
            part.at[far_x, block(b), :], ra.at[b], as_.at[b], ar.at[b],
            x_next if b % 2 == 0 else x_prev,
        )

    def x_copy(k, b):
        return send(
            part.at[sides[k], block(b), :], rx.at[k, block(b), :],
            xs.at[k, b], xr.at[k, b], x_next if k == 0 else x_prev,
        )

    def own_half():
        for t in range(4):
            @pl.when(active(t))
            def _():
                taken(0, t)
                both = lax.dot_general(
                    sc[0], columns(0, t), NT, preferred_element_type=jnp.float32
                )
                part[t] = both[:rows * 4] + both[rows * 4:]

    def compute(b):
        for t in range(4):
            @pl.when(active(t))
            def _():
                if b == 0:
                    taken(1, t)
                both = lax.dot_general(
                    sc[1, b * rows:(b + 1) * rows, :], columns(1, t), NT,
                    preferred_element_type=jnp.float32,
                )
                part[t, block(b), :] = part[t, block(b), :] + (both[:half_rows] + both[half_rows:])

                @pl.when(far_x == t)
                def _():
                    a_copy(b).start()

                @pl.when(sides[1 - b % 2] == t)
                def _():
                    x_copy(1 - b % 2, b).start()

    def relay(b):
        k = b % 2

        @pl.when(active(sides[k]))
        def _():
            a_copy(b).wait_recv()
            part[sides[k], block(b), :] = part[sides[k], block(b), :] + ra[b]
            x_copy(k, b).start()

    def f_copy(b):
        device = (None, y_prev, y_far, y_next)[b // 2]
        return send(fin.at[block(b), :], yb.at[block(b), :], fs.at[b], fr.at[b], device)

    j_own = x * 2 + h
    mine = j_own <= i

    def final(b):
        @pl.when(mine)
        def _():
            x_copy(0, b).wait_recv()
            x_copy(1, b).wait_recv()
            fin[block(b), :] = part[x, block(b), :] + rx[0, block(b), :] + rx[1, block(b), :]
            if b // 2 != 0:
                f_copy(b).start()

    for q in (0, 1):
        y_copy(0, q, 1 if q == 1 else 3, j_ref).wait_recv()
        y_copy(0, q, 2, j_ref).wait_recv()
    for load in loads[1:]:
        load.wait()
    weigh(0)
    scale_own(0, zb[c, 0, 0])
    for s in (1, 2, 3):
        scale_own(s, rb[s - 1, 0])
    for d in (6, 7):
        take(d)
    own_half()
    p_copy(1).wait_recv()
    weigh(1)

    take(8)
    for q in (0, 1):
        @pl.when(first)
        def _():
            c_copy(0, 1 - kind, 8, q).wait_recv()
            y_start(zb.at[0, 1 - kind, 8], q)

    def arrived(b):
        s, q = b // 2, b % 2
        if s == 0:
            src = zb[c, 1 - kind, 8, q * half_rows:(q + 1) * half_rows, :]
        else:
            src = rb[s - 1, 1, q * half_rows:(q + 1) * half_rows, :]
        scale_far(b, src)
        compute(b)

    arrived(0)
    arrived(1)
    y_relay(1, 0)
    arrived(2)
    y_relay(1, 1)
    arrived(7)
    y_copy(1, 1, 1, j_ref).wait_recv()
    arrived(3)
    y_copy(1, 0, 3, j_ref).wait_recv()
    arrived(6)
    relay(0)
    relay(1)
    y_copy(1, 0, 2, j_ref).wait_recv()
    arrived(4)
    y_copy(1, 1, 2, j_ref).wait_recv()
    arrived(5)
    relay(2)
    relay(7)
    relay(3)
    relay(6)
    relay(4)
    relay(5)
    final(2)
    final(7)
    final(3)
    final(6)
    final(0)
    final(1)
    final(4)
    final(5)

    @pl.when(mine)
    def _():
        def place(s, value):
            source = rem(y + s, 4)
            row = ((i * 2 + c) * 4 + y) * rows + lax.broadcasted_iota(jnp.int32, (rows, rows), 0)
            lane = lax.broadcasted_iota(jnp.int32, (rows, rows), 1)
            for k in (0, 1):
                block = (c if k == 0 else 1 - c) * 4 + source
                col = j_own * (rows * 8) + block * rows + lane
                piece = value[:, k * rows:(k + 1) * rows]
                out_ref[:, pl.ds(pl.multiple_of(block * rows, rows), rows)] = jnp.where(
                    col <= row, piece, 0.0
                )

        place(0, fin[0:rows, :])
        for s in (1, 3, 2):
            for q in (0, 1):
                f_copy(s * 2 + q).wait_recv()
            place(s, yb[s * rows:(s + 1) * rows, :])

    @pl.when(j_own > i)
    def _():
        out_ref[...] = jnp.zeros_like(out_ref)

    for k in (0, 1):
        p_copy(k).wait_send()
    e_copy().wait_send()
    for k in (0, 1):
        for way in (0, 1):
            for d in range(1, 9):
                @pl.when(second & sends(k, way, d))
                def _():
                    for p in range(pieces):
                        z_copy(k, way, d, p).wait_send()

                @pl.when(second & handed(k, way, d))
                def _():
                    for q in (0, 1):
                        c_copy(k, way, d, q).wait_send()
    for where in (0, 1):
        for q in (0, 1):
            for s in (1, 2, 3):
                y_copy(where, q, s, j_ref).wait_send()
    @pl.when(active(far_x))
    def _():
        for b in range(8):
            a_copy(b).wait_send()
    for k in (0, 1):
        @pl.when(active(sides[k]))
        def _():
            for b in range(8):
                x_copy(k, b).wait_send()

    @pl.when(mine)
    def _():
        for b in range(2, 8):
            f_copy(b).wait_send()


def on_device(pieces, jacobian, extinction, prior_var):
    rows, vox = jacobian.shape
    width = rows * 8
    dma = pltpu.SemaphoreType.DMA
    vmem = pltpu.VMEM
    f32, bf16 = jnp.float32, jnp.bfloat16
    return pl.pallas_call(
        functools.partial(kernel, pieces),
        out_shape=jax.ShapeDtypeStruct((rows, width), f32),
        in_specs=[
            pl.BlockSpec(memory_space=pl.ANY),
            pl.BlockSpec(memory_space=pl.ANY),
            pl.BlockSpec(memory_space=pl.ANY),
        ],
        out_specs=pl.BlockSpec(memory_space=pltpu.VMEM),
        scratch_shapes=[
            vmem((2, 2, 9, rows, vox), bf16),
            vmem((3, 2, rows, vox), bf16),
            vmem((2, 4), f32),
            vmem((3, 2, vox), f32),
            vmem((4, vox), f32),
            vmem((2, rows * 8, vox), bf16),
            vmem((4, rows * 4, rows * 2), f32),
            vmem((8, rows // 2, rows * 2), f32),
            vmem((2, rows * 4, rows * 2), f32),
            vmem((rows * 4, rows * 2), f32),
            vmem((rows * 4, rows * 2), f32),
            dma((2, 2, 9, pieces)), dma((2, 2, 9, pieces)),
            dma((2, 2, 9, 2)), dma((2, 2, 9, 2)),
            dma, dma,
            dma((2, 2, 3)), dma((2, 2, 3)),
            dma((8,)), dma((8,)),
            dma((2, 8)), dma((2, 8)),
            dma((8,)), dma((8,)),
            dma((2,)), dma((2,)),
            dma((3,)),
        ],
        compiler_params=pltpu.CompilerParams(
            collective_id=0, has_side_effects=True, vmem_limit_bytes=67043328
        ),
    )(jacobian, extinction.T, prior_var)


def solution(mesh):
    return jax.shard_map(
        functools.partial(on_device, 2),
        mesh=mesh,
        in_specs=(P(("row", "wl"), "vox"), P(), P(None, "vox")),
        out_specs=P(("row", "wl"), "vox"),
        check_vma=False,
    )
```
